768 devices in a mesh: gx: 16 (over y_lo, x, core), gy: 48 (over y_hi, z).
Axes of the slice: x: 4, y: 8 (y_hi: 4, y_lo: 2; y = y_hi * 2 + y_lo), z: 12, core: 2. Of those that a mesh axis runs over, the one named last changes fastest.
Arguments:
- positions: float32 [16, 48, 3, 32], P('gx', 'gy'), may hold values from 0 to 12, as said below
- features: float32 [16, 48, 32, 128], P('gx', 'gy'), may hold values from -6 to 6
- cotangent: float32 [16, 48, 32, 1152], P('gx', 'gy'), may hold values from -6 to 6
- nbr_src: int32 [16, 48, 5, 5, 32], P('gx', 'gy'), may hold values from 0 to 31
- nbr_tgt: int32 [16, 48, 5, 5, 32], P('gx', 'gy'), may hold values from 0 to 31
- pair_mask: int32 [16, 48, 5, 5, 32], P('gx', 'gy'), may hold values 0 or 1
- pair_species: int32 [16, 48, 5, 5, 32], P('gx', 'gy'), may hold values from 0 to 9
- w_in: float32 [8, 32], replicated, may hold values from -2 to 2
- species_emb: float32 [10, 32], replicated, may hold values from -6 to 6
- w_out: float32 [32, 384], replicated, may hold values from -1 to 1
Outputs:
- pos_grad: float32 [16, 48, 3, 32], P('gx', 'gy')
- feat_grad: float32 [16, 48, 32, 128], P('gx', 'gy')
The draws below stay inside these ranges and needn't reach their ends.
Inputs may be any that keep to these rules, and one draw needn't show every extreme that they name: `positions`: the first two coordinates lie in 0 to 5, the third in 0 to 12.
All inputs are finite; a program needn't handle non-finite values. No bound on the sum of `pair_mask` on one device may be relied on, other than what follows from the above.
Results may differ from the reference program's by a relative error of at most 0.0003.
Values sent between devices are 32-bit elements; how exact they have to be, the bound alone decides.
A program may use at most 32 MiB of HBM per device.

```python
import math
import jax
import jax.numpy as jnp
from jax import lax

ATOMS = 32
CHANNELS = 128
RBASIS = 8
RHIDDEN = 32
NSPEC = 10
PAIRS = 32
NGX = 16
NGY = 48


def draw_positions(key, part):
    key_plane = jax.random.fold_in(key, 11)
    key_depth = jax.random.fold_in(key, 23)
    plane = jax.random.uniform(key_plane, (NGX, NGY, 2, ATOMS), jnp.float32, 0.0, 5.0)
    depth_extent = float(2 * ATOMS // 5)
    depth = jax.random.uniform(key_depth, (NGX, NGY, 1, ATOMS), jnp.float32, 0.0, depth_extent)
    return jnp.concatenate([plane, depth], axis=2)


def plant(entries, rng, smallest, high):
    place = [jax.random.randint(jax.random.fold_in(rng, axis), (), 0, length) for axis, length in enumerate(entries.shape)]
    longest = entries.shape.index(max(entries.shape))
    neighbour = place[:longest] + [(place[longest] + 1) % entries.shape[longest]] + place[longest + 1:]
    return entries.at[tuple(place)].set(smallest).at[tuple(neighbour)].set(high)


def shard_levels(own_key, dims, cuts, smallest, top_value):
    def one(position, blocks):
        draws = jax.random.uniform(jax.random.fold_in(jax.random.fold_in(own_key, 6), position), (blocks,), jnp.float32, smallest / len(cuts), top_value / len(cuts))
        return jnp.repeat(jnp.exp(draws), dims[position] // blocks).reshape((-1,) + (1,) * (len(dims) - position - 1))

    level = one(*cuts[0])
    for cut in cuts[1:]:
        level = level * one(*cut)
    return level


def centred(rng, shape, width, most, shards=(), kind=jnp.bfloat16):
    entries = width * jax.random.normal(rng, shape, jnp.float32)
    if shards:
        entries = entries * shard_levels(rng, shape, shards, -0.22, 0.18)
    return jnp.clip(entries, -most, most).astype(kind)


def setup_inputs(seed: int = 0) -> dict:
    seeds = jax.random.split(jax.random.key(seed), 11)
    positions = draw_positions(jax.random.fold_in(seeds[10], 71), 0)
    features = centred(seeds[1], (NGX, NGY, ATOMS, CHANNELS), 1.0, 6.0, ((0, 16), (1, 48)), jnp.float32)
    cotangent = centred(seeds[2], (NGX, NGY, ATOMS, 9 * CHANNELS), 1.0, 6.0, ((0, 16), (1, 48)), jnp.float32)
    nbr_src = plant(jax.random.randint(seeds[3], (NGX, NGY, 5, 5, PAIRS), 0, ATOMS), jax.random.fold_in(seeds[3], 1), 0, ATOMS - 1).astype(jnp.int32)
    nbr_tgt = plant(jax.random.randint(seeds[4], (NGX, NGY, 5, 5, PAIRS), 0, ATOMS), jax.random.fold_in(seeds[4], 1), 0, ATOMS - 1).astype(jnp.int32)
    pair_mask = plant((jax.random.randint(seeds[5], (NGX, NGY, 5, 5, PAIRS), 0, 4) < 3).astype(jnp.int32), jax.random.fold_in(seeds[5], 1), 0, 1)
    pair_species = plant(jax.random.randint(seeds[6], (NGX, NGY, 5, 5, PAIRS), 0, NSPEC), jax.random.fold_in(seeds[6], 1), 0, NSPEC - 1).astype(jnp.int32)
    w_in = centred(seeds[7], (RBASIS, RHIDDEN), RBASIS ** -0.5, 2.0, (), jnp.float32)
    species_emb = centred(seeds[8], (NSPEC, RHIDDEN), 1.0, 6.0, (), jnp.float32)
    w_out = centred(seeds[9], (RHIDDEN, 3 * CHANNELS), RHIDDEN ** -0.5, 1.0, (), jnp.float32)
    return dict(positions=positions, features=features, cotangent=cotangent, nbr_src=nbr_src, nbr_tgt=nbr_tgt, pair_mask=pair_mask, pair_species=pair_species, w_in=w_in, species_emb=species_emb, w_out=w_out)


domain_side = 5.0
cutoff = 12.0
soften = 0.25
highest = lax.Precision.HIGHEST

def harmonics(unit):
    unit_x, unit_y, unit_z = (unit[0], unit[1], unit[2])
    root_three = math.sqrt(3.0)
    root_five = math.sqrt(5.0)
    root_fifteen = math.sqrt(15.0)
    return jnp.stack([jnp.ones_like(unit_x), root_three * unit_x, root_three * unit_y, root_three * unit_z, root_fifteen * unit_x * unit_y, root_fifteen * unit_y * unit_z, 0.5 * root_five * (2.0 * unit_z * unit_z - unit_x * unit_x - unit_y * unit_y), root_fifteen * unit_x * unit_z, 0.5 * root_fifteen * (unit_x * unit_x - unit_y * unit_y)], axis=0)

def tile_messages(tgt_pos, src_pos, src_feats, offset, source_index, target_index, live_pair, species, w_in, species_emb, w_out):
    atom_count = tgt_pos.shape[1]
    channels = src_feats.shape[1]
    pair_count = source_index.shape[0]
    relative = jnp.take(src_pos, source_index, axis=1) + offset[:, None] - jnp.take(tgt_pos, target_index, axis=1)
    distance = jnp.sqrt(lax.optimization_barrier(jnp.sum(relative * relative, axis=0)) + soften)
    scaled = distance / cutoff
    envelope = jnp.where(scaled < 1.0, (1.0 - scaled * scaled) ** 2, 0.0) * live_pair.astype(jnp.float32)
    orders = jnp.arange(1, w_in.shape[0] + 1, dtype=jnp.int32).astype(jnp.float32)
    radial_basis = math.sqrt(2.0 / cutoff) * jnp.sin(orders[None, :] * math.pi * scaled[:, None]) / distance[:, None]
    picked = (species[:, None] == jnp.arange(species_emb.shape[0], dtype=jnp.int32)[None, :]).astype(jnp.float32)
    hidden = jax.nn.silu(jnp.dot(radial_basis, w_in, precision=highest) + jnp.dot(picked, species_emb, precision=highest))
    radial = jnp.dot(hidden, w_out, precision=highest).reshape(pair_count, 3, channels) * envelope[:, None, None]
    radial_full = jnp.concatenate([radial[:, 0:1], jnp.repeat(radial[:, 1:2], 3, axis=1), jnp.repeat(radial[:, 2:3], 5, axis=1)], axis=1)
    shapes = harmonics(relative / distance[None, :])
    gathered = jnp.take(src_feats, source_index, axis=0)
    message = radial_full * shapes.T[:, :, None] * gathered[:, None, :]
    return jax.ops.segment_sum(message.reshape(pair_count, 9 * channels), target_index, num_segments=atom_count)

def tile_grads(tgt_pos, src_pos, src_feats, offset, source_index, target_index, live_pair, species, w_in, species_emb, w_out, cot_block):

    def forward(target_xyz, source_xyz, source_vals):
        return tile_messages(target_xyz, source_xyz, source_vals, offset, source_index, target_index, live_pair, species, w_in, species_emb, w_out)
    pullback = jax.vjp(forward, tgt_pos, src_pos, src_feats)[1]
    return pullback(cot_block)

def reference(positions, features, cotangent, nbr_src, nbr_tgt, pair_mask, pair_species, w_in, species_emb, w_out):
    grid_x = positions.shape[0]
    grid_y = positions.shape[1]

    def visit(running, flat_index):
        pos_total, feat_total = running
        cell_a = flat_index // grid_y
        cell_b = flat_index % grid_y
        for row_step in range(-2, 3):
            for col_step in range(-2, 3):
                src_a = (cell_a + row_step) % grid_x
                tgt_b = (cell_b + col_step) % grid_y
                offset = jnp.array([row_step * domain_side, -col_step * domain_side, 0.0], dtype=jnp.float32)
                grads = tile_grads(positions[cell_a, tgt_b], positions[src_a, cell_b], features[src_a, cell_b], offset, nbr_src[cell_a, cell_b, row_step + 2, col_step + 2], nbr_tgt[cell_a, cell_b, row_step + 2, col_step + 2], pair_mask[cell_a, cell_b, row_step + 2, col_step + 2], pair_species[cell_a, cell_b, row_step + 2, col_step + 2], w_in, species_emb, w_out, cotangent[cell_a, tgt_b])
                pos_total = pos_total.at[cell_a, tgt_b].add(grads[0])
                pos_total = pos_total.at[src_a, cell_b].add(grads[1])
                feat_total = feat_total.at[src_a, cell_b].add(grads[2])
        return ((pos_total, feat_total), None)
    start = (jnp.zeros(positions.shape, jnp.float32), jnp.zeros(features.shape, jnp.float32))
    finals = lax.scan(visit, start, jnp.arange(grid_x * grid_y, dtype=jnp.int32))[0]
    return (finals[0], finals[1])
```

```python
import math

import jax
import jax.numpy as jnp
from jax import lax
from jax.experimental import pallas as pl
from jax.experimental.pallas import tpu as pltpu
from jax.sharding import PartitionSpec as P

MESH = pl.DeviceIdType.MESH
SIDE = 5.0
CUTOFF = 12.0
SOFTEN = 0.25
LANES = 256
F32 = jnp.float32
BF16 = jnp.bfloat16
NN = (((1,), (0,)), ((), ()))
NT = (((1,), (1,)), ((), ()))
TN = (((0,), (0,)), ((), ()))
HIGHEST = lax.Precision.HIGHEST
STEPS = (-2, -1, 0, 1, 2)
AWAY = (-1, 1, -2, 2)


def dot(lhs, rhs, dims):
    return lax.dot_general(lhs, rhs, dims, preferred_element_type=F32)


def exact_dot(lhs, rhs, dims):
    return lax.dot_general(lhs, rhs, dims, precision=HIGHEST, preferred_element_type=F32)


def split2(value):
    high = value.astype(BF16).astype(F32)
    return high, value - high


def split3(value):
    high, rest = split2(value)
    middle, low = split2(rest)
    return high, middle, low


def sin_cos_pi(x):
    turns = jnp.floor(x + 0.5)
    y = (x - turns) * math.pi
    half = turns * 0.5
    sign = 1.0 - 4.0 * (half - jnp.floor(half))
    y2 = y * y
    s = -1.0 / 39916800.0 + y2 * (1.0 / 6227020800.0)
    for c in (1.0 / 362880.0, -1.0 / 5040.0, 1.0 / 120.0, -1.0 / 6.0, 1.0):
        s = s * y2 + c
    c_ = 1.0 / 479001600.0 - y2 * (1.0 / 87178291200.0)
    for c in (-1.0 / 3628800.0, 1.0 / 40320.0, -1.0 / 720.0, 1.0 / 24.0, -0.5, 1.0):
        c_ = c_ * y2 + c
    return s * y * sign, c_ * sign


def kernel(
    pos_in, feat_in, cot_in, src_in, tgt_in, mask_in, spec_in, w_in, emb, w_out,
    pos_out, feat_out,
    posx, posy, feats, cots, lists, index, posmat, onehot, gath, fbuf, radial, wt, featt,
    sph, rows, pp, acc, tgt_send, ret, tgt_ret,
    local_sem, fx_send, fx_recv, py_send, py_recv, px_send, px_recv, ct_send, ct_recv,
    rs_send, rs_recv, rt_send, rt_recv,
):
    a, b = lax.axis_index("gx"), lax.axis_index("gy")
    na, nb = lax.axis_size("gx"), lax.axis_size("gy")
    along_x = {s: (lax.rem(a + s + na, na), b) for s in STEPS}
    along_y = {s: (a, lax.rem(b + s + nb, nb)) for s in STEPS}

    barrier = pltpu.get_barrier_semaphore()
    for s in AWAY:
        pl.semaphore_signal(barrier, inc=1, device_id=along_x[s], device_id_type=MESH)
        pl.semaphore_signal(barrier, inc=1, device_id=along_y[s], device_id_type=MESH)

    own = [
        pltpu.make_async_copy(src_in.at[0, 0], lists.at[0], local_sem.at[0]),
        pltpu.make_async_copy(tgt_in.at[0, 0], lists.at[1], local_sem.at[1]),
        pltpu.make_async_copy(mask_in.at[0, 0], lists.at[2], local_sem.at[2]),
        pltpu.make_async_copy(spec_in.at[0, 0], lists.at[3], local_sem.at[3]),
        pltpu.make_async_copy(pos_in.at[0, 0], posx.at[2], local_sem.at[4]),
        pltpu.make_async_copy(pos_in.at[0, 0], posy.at[2], local_sem.at[5]),
        pltpu.make_async_copy(feat_in.at[0, 0], feats.at[2], local_sem.at[6]),
        pltpu.make_async_copy(cot_in.at[0, 0], cots.at[2], local_sem.at[7]),
    ]
    for copy in own:
        copy.start()

    pl.semaphore_wait(barrier, 8)

    def send(src, dst, send_sem, recv_sem, device):
        copy = pltpu.make_async_remote_copy(
            src_ref=src, dst_ref=dst, send_sem=send_sem, recv_sem=recv_sem, device_id=device, device_id_type=MESH
        )
        copy.start()
        return copy

    sent_px, sent_py, sent_fx, sent_ct = {}, {}, {}, {}
    for s in AWAY:
        i = s + 2
        sent_px[s] = send(pos_in.at[0, 0], posx.at[i], px_send.at[i], px_recv.at[i], along_x[-s])
        sent_py[s] = send(pos_in.at[0, 0], posy.at[i], py_send.at[i], py_recv.at[i], along_y[-s])
    for s in AWAY:
        i = s + 2
        sent_ct[s] = send(cot_in.at[0, 0], cots.at[i], ct_send.at[i], ct_recv.at[i], along_y[-s])
        sent_fx[s] = send(feat_in.at[0, 0], feats.at[i], fx_send.at[i], fx_recv.at[i], along_x[-s])

    for copy in own:
        copy.wait()
    index[...] = jnp.zeros_like(index)
    for i in range(5):
        for field in range(4):
            index[field, 0:5, 32 * i : 32 * i + 32] = lists[field, i]
    lane = lax.broadcasted_iota(jnp.int32, (8, LANES), 1)
    group = lane // 32
    src_rows = jnp.where(lane < 160, index[0] + 32 * group, -1)
    tgt_rows = jnp.where(lane < 160, index[1] + 160, -1)
    alive = index[2].astype(F32)
    species = index[3]

    src_ids = lax.broadcasted_iota(jnp.int32, (160, LANES), 0)
    tgt_ids = lax.broadcasted_iota(jnp.int32, (32, LANES), 0) + 160
    for j in range(5):
        onehot[j, 0:160] = (src_ids == src_rows[j : j + 1]).astype(F32).astype(BF16)
        onehot[j, 160:192] = (tgt_ids == tgt_rows[j : j + 1]).astype(F32).astype(BF16)

    w_high, w_low = split2(w_out[...])
    wt[...] = jnp.concatenate([w_high, w_high, w_low], axis=0).T.astype(BF16)

    for s in AWAY:
        sent_px[s].wait_recv()
        sent_py[s].wait_recv()
    posmat[...] = jnp.zeros_like(posmat)
    for i in range(5):
        posmat[0:3, 32 * i : 32 * i + 32] = posx[i]
    rel = []
    for j in range(5):
        posmat[0:3, 160:192] = -posy[j]
        pieces = jnp.concatenate(split3(posmat[...]), axis=0).astype(BF16)
        picked = dot(pieces, onehot[j], NN)
        rel.append(picked[0:8] + picked[8:16] + picked[16:24])
    step_row = lax.broadcasted_iota(jnp.int32, (8, LANES), 0)
    pad = [jnp.zeros((1, LANES), F32)] * 3
    rx = jnp.concatenate([r[0:1] for r in rel] + pad, axis=0) + (group - 2).astype(F32) * SIDE
    ry = jnp.concatenate([r[1:2] for r in rel] + pad, axis=0) - (step_row - 2).astype(F32) * SIDE
    rz = jnp.concatenate([r[2:3] for r in rel] + pad, axis=0)
    dist = jnp.sqrt(rx * rx + ry * ry + rz * rz + SOFTEN)
    inv = 1.0 / dist
    ux, uy, uz = rx * inv, ry * inv, rz * inv
    q = dist * (1.0 / CUTOFF)
    left = jnp.maximum(1.0 - q * q, 0.0)
    env = left * left * alive
    denv = q * left * alive * (-4.0 / CUTOFF)
    r3, r5, r15 = math.sqrt(3.0), math.sqrt(5.0), math.sqrt(15.0)
    for m, y in enumerate(
        (
            r3 * ux, r3 * uy, r3 * uz,
            r15 * ux * uy, r15 * uy * uz, 0.5 * r5 * (2.0 * uz * uz - ux * ux - uy * uy),
            r15 * ux * uz, 0.5 * r15 * (ux * ux - uy * uy),
        )
    ):
        sph[m] = y
    for k, value in enumerate((ux, uy, uz, inv)):
        rows[k] = value

    order = (lax.broadcasted_iota(jnp.int32, (8, LANES), 0) + 1).astype(F32)
    spec_ids = lax.broadcasted_iota(jnp.int32, (10, LANES), 0)
    root = math.sqrt(2.0 / CUTOFF)
    for j in range(5):
        inv_j, env_j, denv_j = inv[j : j + 1], env[j : j + 1], denv[j : j + 1]
        sine, cosine = sin_cos_pi(order * q[j : j + 1])
        basis = root * sine * inv_j
        dbasis = (order * (root * math.pi / CUTOFF) * cosine - basis) * inv_j
        chosen = (spec_ids == species[j : j + 1]).astype(F32)
        both = exact_dot(w_in[...], jnp.concatenate([basis, dbasis], axis=1), TN)
        z = both[:, 0:LANES] + exact_dot(emb[...], chosen, TN)
        dz = both[:, LANES:]
        sig = 1.0 / (1.0 + jnp.exp(-z))
        hidden = z * sig
        dhidden = sig * (1.0 + z * (1.0 - sig)) * dz
        stacked = jnp.concatenate([hidden * env_j, dhidden * env_j + hidden * denv_j], axis=1)
        high, low = split2(stacked)
        radial[j] = dot(wt[...], jnp.concatenate([high, low, high], axis=0).astype(BF16), NN)

    for s in AWAY:
        sent_fx[s].wait_recv()
    all_feats = jnp.concatenate([feats[i] for i in range(5)], axis=0)
    f_high, f_low = split2(all_feats)
    featt[...] = jnp.concatenate([f_high, f_low], axis=1).T.astype(BF16)
    for j in range(5):
        two = dot(featt[...], onehot[j, 0:160], NN)
        fbuf[j] = two[0:128] + two[128:256]

    acc[...] = jnp.zeros_like(acc)

    for s in (0, -1, 1, -2, 2):
        j = s + 2
        if s != 0:
            sent_ct[s].wait_recv()
        c_high, c_low = split2(cots[j])
        target_hot = onehot[j, 160:192]
        gath[...] = dot(
            jnp.concatenate([c_high, c_low], axis=0).astype(BF16).T, jnp.concatenate([target_hot, target_hot], axis=0), NN
        )

        def channels(c, carry, j=j):
            r0 = pl.multiple_of(c * 8, 8)
            f = fbuf[j, pl.ds(r0, 8), :]
            g = [gath[pl.ds(m * 128 + r0, 8), :] for m in range(9)]
            y = [None] + [sph[m, j : j + 1, :] for m in range(8)]
            rad = [radial[j, pl.ds(l * 128 + r0, 8), 0:LANES] for l in range(3)]
            drad = [radial[j, pl.ds(l * 128 + r0, 8), LANES : 2 * LANES] for l in range(3)]
            c1 = y[1] * g[1] + y[2] * g[2] + y[3] * g[3]
            c2 = y[4] * g[4] + y[5] * g[5] + y[6] * g[6] + y[7] * g[7] + y[8] * g[8]
            pp[pl.ds(r0, 8), :] = rad[0] * g[0] + rad[1] * c1 + rad[2] * c2
            p1, p2 = rad[1] * f, rad[2] * f
            out = [carry[0] + f * (drad[0] * g[0] + drad[1] * c1 + drad[2] * c2)]
            for m in range(1, 9):
                out.append(carry[m] + (p1 if m < 4 else p2) * g[m])
            return tuple(out)

        start = tuple(jnp.zeros((8, LANES), F32) for _ in range(9))
        sums = lax.fori_loop(0, 16, channels, start)
        gd, *gy = [jnp.sum(v, axis=0, keepdims=True) for v in sums]
        ux_j, uy_j, uz_j, inv_j = (rows[k, j : j + 1, :] for k in range(4))
        gux = r3 * gy[0] + r15 * (uy_j * gy[3] + uz_j * gy[6] + ux_j * gy[7]) - r5 * ux_j * gy[5]
        guy = r3 * gy[1] + r15 * (ux_j * gy[3] + uz_j * gy[4] - uy_j * gy[7]) - r5 * uy_j * gy[5]
        guz = r3 * gy[2] + r15 * (uy_j * gy[4] + ux_j * gy[6]) + 2.0 * r5 * uz_j * gy[5]
        along = gd - (gux * ux_j + guy * uy_j + guz * uz_j) * inv_j
        grad = jnp.concatenate(
            [gux * inv_j + along * ux_j, guy * inv_j + along * uy_j, guz * inv_j + along * uz_j]
            + [jnp.zeros((5, LANES), F32)],
            axis=0,
        )
        scat = dot(jnp.concatenate(split2(grad), axis=0).astype(BF16), onehot[j], NT)
        scat = scat[0:8] + scat[8:16]
        p_high, p_low = split2(pp[...])
        fscat = dot(onehot[j, 0:160], jnp.concatenate([p_high, p_low], axis=0).astype(BF16), NT)
        fscat = fscat[:, 0:128] + fscat[:, 128:256]
        for i in range(5):
            acc[i, 0:32, :] += fscat[32 * i : 32 * i + 32]
            acc[i, 32:40, 0:32] += scat[:, 32 * i : 32 * i + 32]
        tgt_send[j, :, 0:32] = -scat[:, 160:192]

    sent_rs, sent_rt = {}, {}
    for s in AWAY:
        i = s + 2
        sent_rt[s] = send(tgt_send.at[i], tgt_ret.at[i], rt_send.at[i], rt_recv.at[i], along_y[s])
        sent_rs[s] = send(acc.at[i], ret.at[i], rs_send.at[i], rs_recv.at[i], along_x[s])

    pos_total = acc[2, 32:40, :] + tgt_send[2]
    feat_total = acc[2, 0:32, :]
    for s in AWAY:
        i = s + 2
        sent_rs[s].wait_recv()
        feat_total = feat_total + ret[i, 0:32, :]
        pos_total = pos_total + ret[i, 32:40, :]
    feat_out[0, 0] = feat_total
    for s in AWAY:
        sent_rt[s].wait_recv()
        pos_total = pos_total + tgt_ret[s + 2]
    pos_out[0, 0] = pos_total[0:3, 0:32]
    for s in AWAY:
        for sent in (sent_px, sent_py, sent_fx, sent_ct, sent_rs, sent_rt):
            sent[s].wait_send()


def local(positions, features, cotangent, nbr_src, nbr_tgt, pair_mask, pair_species, w_in, species_emb, w_out):
    hbm = pl.BlockSpec(memory_space=pl.ANY)
    vmem = pl.BlockSpec(memory_space=pltpu.VMEM)
    dma = pltpu.SemaphoreType.DMA
    return pl.pallas_call(
        kernel,
        out_shape=(
            jax.ShapeDtypeStruct(positions.shape, F32),
            jax.ShapeDtypeStruct(features.shape, F32),
        ),
        in_specs=[hbm] * 7 + [vmem] * 3,
        out_specs=(vmem, vmem),
        scratch_shapes=[
            pltpu.VMEM((5, 3, 32), F32),
            pltpu.VMEM((5, 3, 32), F32),
            pltpu.VMEM((5, 32, 128), F32),
            pltpu.VMEM((5, 32, 1152), F32),
            pltpu.VMEM((4, 5, 5, 32), jnp.int32),
            pltpu.VMEM((4, 8, LANES), jnp.int32),
            pltpu.VMEM((8, 192), F32),
            pltpu.VMEM((5, 192, LANES), BF16),
            pltpu.VMEM((1152, LANES), F32),
            pltpu.VMEM((5, 128, LANES), F32),
            pltpu.VMEM((5, 384, 2 * LANES), F32),
            pltpu.VMEM((384, 96), BF16),
            pltpu.VMEM((256, 160), BF16),
            pltpu.VMEM((8, 8, LANES), F32),
            pltpu.VMEM((4, 8, LANES), F32),
            pltpu.VMEM((128, LANES), F32),
            pltpu.VMEM((5, 40, 128), F32),
            pltpu.VMEM((5, 8, 128), F32),
            pltpu.VMEM((5, 40, 128), F32),
            pltpu.VMEM((5, 8, 128), F32),
            dma((8,)),
        ]
        + [dma((5,))] * 12,
        compiler_params=pltpu.CompilerParams(collective_id=0, has_side_effects=True, vmem_limit_bytes=48 * 2**20),
    )(positions, features, cotangent, nbr_src, nbr_tgt, pair_mask, pair_species, w_in, species_emb, w_out)


def solution(mesh):
    grid = P("gx", "gy", None, None)
    lists = P("gx", "gy", None, None, None)
    return jax.shard_map(
        local,
        mesh=mesh,
        in_specs=(grid, grid, grid, lists, lists, lists, lists, P(), P(), P()),
        out_specs=(grid, grid),
        check_vma=False,
    )
```

```python
import math

import jax
import jax.numpy as jnp
from jax import lax
from jax.experimental import pallas as pl
from jax.experimental.pallas import tpu as pltpu
from jax.sharding import PartitionSpec as P

MESH = pl.DeviceIdType.MESH
SIDE = 5.0
CUTOFF = 12.0
SOFTEN = 0.25
F32 = jnp.float32
BF16 = jnp.bfloat16
NN = (((1,), (0,)), ((), ()))
NT = (((1,), (1,)), ((), ()))
AWAY = (-1, 1, -2, 2)
PARTS = 9
UNROLL = 16
COUNT = (1, 2, 2)
LANES = (256, 384, 384)
R3, R5, R15 = math.sqrt(3.0), math.sqrt(5.0), math.sqrt(15.0)


def dot(lhs, rhs, dims):
    return lax.dot_general(lhs, rhs, dims, preferred_element_type=F32)


def split2(value):
    high = value.astype(BF16).astype(F32)
    return high, value - high


def split3(value):
    high, rest = split2(value)
    middle, low = split2(rest)
    return high, middle, low


def sin_cos_pi(x):
    turns = jnp.floor(x + 0.5)
    y = (x - turns) * math.pi
    half = turns * 0.5
    sign = 1.0 - 4.0 * (half - jnp.floor(half))
    y2 = y * y
    s = -1.0 / 39916800.0 + y2 * (1.0 / 6227020800.0)
    for c in (1.0 / 362880.0, -1.0 / 5040.0, 1.0 / 120.0, -1.0 / 6.0, 1.0):
        s = s * y2 + c
    c_ = 1.0 / 479001600.0 - y2 * (1.0 / 87178291200.0)
    for c in (-1.0 / 3628800.0, 1.0 / 40320.0, -1.0 / 720.0, 1.0 / 24.0, -0.5, 1.0):
        c_ = c_ * y2 + c
    return s * y * sign, c_ * sign


def run_length(peers):
    return 12 if peers % 12 == 0 else 4


def remote(src, dst, send_sem, recv_sem, device):
    return pltpu.make_async_remote_copy(
        src_ref=src, dst_ref=dst, send_sem=send_sem, recv_sem=recv_sem, device_id=device, device_id_type=MESH
    )


def piece(ref, k):
    width = ref.shape[-1] // PARTS
    return ref.at[:, pl.ds(k * width, width)]


def kernel(
    pos_in, feat_in, cot_in, src_in, tgt_in, mask_in, spec_in, w_in_hbm, emb_hbm, w_out_hbm,
    pos_out, feat_out,
    w_in, emb, w_out, posx, posy, feats, cots, lists, wt, w_first, featt, acc, tgt_send, ret, tgt_ret, way,
    index0, index1, index2, hot0, hot1, hot2, posmat0, posmat1, posmat2, gath0, gath1, gath2,
    fbuf0, fbuf1, fbuf2, radial0, radial1, radial2, sph0, sph1, sph2, geo0, geo1, geo2, pp0, pp1, pp2,
    local_sem, fx_send, fx_recv, py_send, py_recv, px_send, px_recv, ct_send, ct_recv,
    rs_send, rs_recv, rt_send, rt_recv, w_send, w_recv, r_send, r_recv, crossed,
    st_send, st_recv, fw_send, stage_pos, m_send, m_recv, passed,
):
    index, hot, posmat = (index0, index1, index2), (hot0, hot1, hot2), (posmat0, posmat1, posmat2)
    gath, fbuf, radial = (gath0, gath1, gath2), (fbuf0, fbuf1, fbuf2), (radial0, radial1, radial2)
    sph, geo, pp = (sph0, sph1, sph2), (geo0, geo1, geo2), (pp0, pp1, pp2)
    a, b = lax.axis_index("gx"), lax.axis_index("gy")
    na, nb = lax.axis_size("gx"), lax.axis_size("gy")
    run = run_length(nb)
    place = lax.rem(b, run)
    low = place < run // 2
    far = jnp.where(low, -1, 1)

    def x_at(shift):
        return (lax.rem(a + shift + na, na), b)

    def y_at(shift):
        return (a, lax.rem(b + shift + nb, nb))

    def slots(g):
        return [2] if g == 0 else [2 - far, 2 - 2 * far] if g == 1 else [2 + far, 2 + 2 * far]

    barrier = pltpu.get_barrier_semaphore()

    def signal(semaphore, device):
        pl.semaphore_signal(semaphore, inc=1, device_id=device, device_id_type=MESH)

    for s in AWAY:
        signal(barrier, x_at(s))
    for s in (-2, -1):
        signal(barrier, y_at(s))
    for s in (1, 2):
        @pl.when(place + s < run)
        def _(s=s):
            signal(barrier, y_at(s))

    for p, shifts in ((0, (run, run - 1, run - 2)), (1, (run, run - 2, -3))):
        @pl.when(place == p)
        def _(shifts=shifts):
            for shift in shifts:
                signal(barrier, y_at(shift))

    entered = jnp.where(place == 0, 7, jnp.where(place >= run - 2, 10, 8))

    own = [
        pltpu.make_async_copy(src, dst, local_sem.at[k])
        for k, (src, dst) in enumerate(
            (
                (src_in, lists.at[0]), (tgt_in, lists.at[1]), (mask_in, lists.at[2]), (spec_in, lists.at[3]),
                (w_out_hbm, w_out), (w_in_hbm, w_in), (emb_hbm, emb), (cot_in.at[0, 0], cots.at[2]),
                (pos_in, posx.at[2]), (pos_in, posy.at[2]), (feat_in.at[0, 0], feats.at[2]),
            )
        )
    ]
    for copy in own:
        copy.start()

    def straight(k):
        return remote(piece(cot_in.at[0, 0], k), piece(cots.at[1], k), m_send.at[k], m_recv.at[k], y_at(1))

    def to_way(k):
        return remote(piece(cot_in.at[0, 0], k), piece(passed, k), w_send.at[k], w_recv.at[k], y_at(3))

    def pass_on(p, k):
        src = cots.at[1] if p == 0 else passed
        return remote(piece(src, k), piece(cots.at[0], k), r_send.at[k], r_recv.at[k], y_at(1 - 2 * p))

    def of_pos_x(s):
        return remote(pos_in, posx.at[s + 2], px_send.at[s + 2], px_recv.at[s + 2], x_at(-s))

    def of_feats(s):
        return remote(feat_in.at[0, 0], feats.at[s + 2], fx_send.at[s + 2], fx_recv.at[s + 2], x_at(-s))

    def of_pos_y(slot):
        return remote(pos_in, posy.at[slot], py_send.at[slot], py_recv.at[slot], y_at(2 - slot))

    def of_cot(slot):
        return remote(cot_in.at[0, 0], cots.at[slot], ct_send.at[slot], ct_recv.at[slot], y_at(2 - slot))

    def of_sums(s):
        return remote(acc.at[s + 2], ret.at[s + 2], rs_send.at[s + 2], rs_recv.at[s + 2], x_at(s))

    def of_targets(slot):
        return remote(tgt_send.at[slot], tgt_ret.at[slot], rt_send.at[slot], rt_recv.at[slot], y_at(slot - 2))

    def gathered_cot(g):
        pieces = [split2(cots[j]) for j in slots(g)]
        stacked = jnp.concatenate([p[0] for p in pieces] + [p[1] for p in pieces], axis=0).astype(BF16)
        target_hot = hot[g][160 : 160 + 32 * COUNT[g]]
        gath[g][...] = dot(stacked.T, jnp.concatenate([target_hot, target_hot], axis=0), NN)

    def lane_maps(g):
        lane = lax.broadcasted_iota(jnp.int32, (1, LANES[g]), 1)
        second = jnp.where(lane >= 160, 1, 0)
        return lane < 160 * COUNT[g], second, (lane - 160 * second) // 32

    def setup():
        for copy in own[:8]:
            copy.wait()
        for g in range(3):
            index[g][...] = jnp.zeros_like(index[g])
            for t, j in enumerate(slots(g)):
                for i in range(5):
                    at = 160 * t + 32 * i
                    for field in range(4):
                        index[g][field : field + 1, at : at + 32] = lists[field, 5 * i + j]
            used, second, step = lane_maps(g)
            src_row = jnp.where(used, index[g][0:1] + 32 * step, -1)
            tgt_row = jnp.where(used, index[g][1:2] + 32 * second + 160, -1)
            src_ids = lax.broadcasted_iota(jnp.int32, (160, LANES[g]), 0)
            tgt_ids = lax.broadcasted_iota(jnp.int32, (32 * COUNT[g], LANES[g]), 0) + 160
            hot[g][0:160] = (src_ids == src_row).astype(F32).astype(BF16)
            hot[g][160:] = (tgt_ids == tgt_row).astype(F32).astype(BF16)
        w_high, w_low = split2(w_out[...])
        wt[...] = jnp.concatenate([w_high, w_high, w_low], axis=0).T.astype(BF16)
        i_high, i_low = split2(w_in[...])
        e_high, e_low = split2(emb[...])
        gap = jnp.zeros((6, 32), F32)
        first = [i_high, i_high, i_low, e_high, gap, e_low, gap, jnp.zeros((8, 32), F32)]
        w_first[...] = jnp.concatenate(first, axis=0).T.astype(BF16)
        gathered_cot(0)

    pl.when(low)(setup)
    pl.semaphore_wait(barrier, entered)

    @pl.when(place == run - 1)
    def _():
        signal(crossed, y_at(1 - run))
        signal(crossed, y_at(2 - run))

    @pl.when(place == run - 2)
    def _():
        signal(crossed, y_at(2 - run))

    def whole(slot):
        kept = place + 2 - slot >= 0
        if slot == 0:
            return place < run - 2
        return place < run - 1 if slot == 1 else kept

    for slot in (0, 4, 1, 3):
        @pl.when(place + 2 - slot >= 0)
        def _(slot=slot):
            of_pos_y(slot).start()
    for s in AWAY:
        of_pos_x(s).start()
    for s in AWAY:
        of_feats(s).start()
    for p, copy in ((run - 1, straight), (run - 2, to_way)):
        @pl.when(place == p)
        def _(copy=copy):
            for k in range(PARTS):
                copy(k).start()
    for slot in (0, 4, 1, 3):
        @pl.when(whole(slot))
        def _(slot=slot):
            of_cot(slot).start()

    def stage(k):
        src, dst = ((pos_in, stage_pos), (cot_in.at[0, 0], way))[k]
        return remote(src, dst, st_send.at[k], st_recv.at[k], y_at(-run))

    def forward(k, slot, n, shift):
        src, dst = ((stage_pos, posy.at[slot]), (way, cots.at[slot]))[k]
        return remote(src, dst, fw_send.at[2 * n + k], (py_recv, ct_recv)[k].at[slot], y_at(shift))

    forwards = {0: ((3, run - 1), (4, run - 2)), 1: ((4, run - 2),)}

    @pl.when(place <= 1)
    def _():
        stage(0).start()
        stage(1).start()

    def cross():
        for p, receivers in forwards.items():
            @pl.when(place == p)
            def _(receivers=receivers):
                pl.semaphore_wait(crossed, len(receivers))
                for k in range(2):
                    stage(k).wait_recv()
                    for n, (slot, shift) in enumerate(receivers):
                        forward(k, slot, n, shift).start()

    pl.when(jnp.logical_not(low))(setup)

    def geometry(g):
        width = LANES[g]
        for t, j in enumerate(slots(g)):
            posmat[g][0:3, 160 + 32 * t : 192 + 32 * t] = -posy[j, :, 0]
        picked = dot(jnp.concatenate(split3(posmat[g][...]), axis=0).astype(BF16), hot[g][...], NN)
        picked = picked[0:8] + picked[8:16] + picked[16:24]
        used, second, step = lane_maps(g)
        rx = picked[0:1] + (step - 2).astype(F32) * SIDE
        ry, rz = picked[1:2], picked[2:3]
        if g:
            ry = ry - ((far if g == 2 else -far) * (1 + second)).astype(F32) * SIDE
        dist = jnp.sqrt(rx * rx + ry * ry + rz * rz + SOFTEN)
        inv = 1.0 / dist
        ux, uy, uz = rx * inv, ry * inv, rz * inv
        q = dist * (1.0 / CUTOFF)
        left = jnp.maximum(1.0 - q * q, 0.0)
        alive = index[g][2:3].astype(F32)
        env = left * left * alive
        denv = q * left * alive * (-4.0 / CUTOFF)
        sph[g][...] = jnp.concatenate(
            [
                R3 * ux, R3 * uy, R3 * uz,
                R15 * ux * uy, R15 * uy * uz, 0.5 * R5 * (2.0 * uz * uz - ux * ux - uy * uy),
                R15 * ux * uz, 0.5 * R15 * (ux * ux - uy * uy),
            ],
            axis=0,
        )
        geo[g][0:4] = jnp.concatenate([ux, uy, uz, inv], axis=0)
        order = (lax.broadcasted_iota(jnp.int32, (8, width), 0) + 1).astype(F32)
        root = math.sqrt(2.0 / CUTOFF)
        sine, cosine = sin_cos_pi(order * q)
        basis = root * sine * inv
        dbasis = (order * (root * math.pi / CUTOFF) * cosine - basis) * inv
        chosen = (lax.broadcasted_iota(jnp.int32, (16, width), 0) == index[g][3:4]).astype(F32)
        chosen = jnp.concatenate([chosen, jnp.zeros_like(chosen)], axis=1)
        high, rest = split2(jnp.concatenate([basis, dbasis], axis=1))
        first = jnp.concatenate([high, rest, high, chosen, chosen, jnp.zeros_like(high)], axis=0)
        both = dot(w_first[...], first.astype(BF16), NN)
        z, dz = both[:, :width], both[:, width:]
        sig = 1.0 / (1.0 + jnp.exp(-z))
        hidden = z * sig
        dhidden = sig * (1.0 + z * (1.0 - sig)) * dz
        high, rest = split2(jnp.concatenate([hidden * env, dhidden * env + hidden * denv], axis=1))
        radial[g][...] = dot(wt[...], jnp.concatenate([high, rest, high], axis=0).astype(BF16), NN)

    def main(g):
        width = LANES[g]
        columns = []
        for block in range(width // 128):
            at = 128 * block
            lanes = pl.ds(at, 128)

            def channels(c, carry, at=at, lanes=lanes):
                carry = list(carry)
                products = []
                for u in range(UNROLL):
                    r0 = pl.multiple_of(c * (8 * UNROLL) + u * 8, 8)
                    f = fbuf[g][pl.ds(r0, 8), lanes]
                    w = [gath[g][pl.ds(m * 128 + r0, 8), lanes] for m in range(9)]
                    y = [None] + [sph[g][m : m + 1, lanes] for m in range(8)]
                    rad = [radial[g][pl.ds(l * 128 + r0, 8), lanes] for l in range(3)]
                    drad = [radial[g][pl.ds(l * 128 + r0, 8), pl.ds(width + at, 128)] for l in range(3)]
                    c1 = y[1] * w[1] + y[2] * w[2] + y[3] * w[3]
                    c2 = (y[4] * w[4] + y[5] * w[5]) + (y[6] * w[6] + y[7] * w[7]) + y[8] * w[8]
                    products.append(rad[0] * w[0] + rad[1] * c1 + rad[2] * c2)
                    p1, p2 = rad[1] * f, rad[2] * f
                    carry[0] = carry[0] + f * (drad[0] * w[0] + drad[1] * c1 + drad[2] * c2)
                    for m in range(1, 9):
                        carry[m] = carry[m] + (p1 if m < 4 else p2) * w[m]
                for u in range(UNROLL):
                    pp[g][pl.ds(pl.multiple_of(c * (8 * UNROLL) + u * 8, 8), 8), lanes] = products[u]
                return tuple(carry)

            sums = lax.fori_loop(0, 16 // UNROLL, channels, tuple(jnp.zeros((8, 128), F32) for _ in range(9)))
            columns.append([jnp.sum(v, axis=0, keepdims=True) for v in sums])
        gd, *gy = [jnp.concatenate([column[m] for column in columns], axis=1) for m in range(9)]
        ux, uy, uz, inv = (geo[g][k : k + 1] for k in range(4))
        gux = R3 * gy[0] + R15 * (uy * gy[3] + uz * gy[6] + ux * gy[7]) - R5 * ux * gy[5]
        guy = R3 * gy[1] + R15 * (ux * gy[3] + uz * gy[4] - uy * gy[7]) - R5 * uy * gy[5]
        guz = R3 * gy[2] + R15 * (uy * gy[4] + ux * gy[6]) + 2.0 * R5 * uz * gy[5]
        along = gd - (gux * ux + guy * uy + guz * uz) * inv
        grad = jnp.concatenate(
            [gux * inv + along * ux, guy * inv + along * uy, guz * inv + along * uz, jnp.zeros((5, width), F32)], axis=0
        )
        scat = dot(jnp.concatenate(split2(grad), axis=0).astype(BF16), hot[g][...], NT)
        scat = scat[0:8] + scat[8:16]
        for t, j in enumerate(slots(g)):
            tgt_send[j, :, 0:32] = -scat[:, 160 + 32 * t : 192 + 32 * t]
        p_high, p_low = split2(pp[g][...])
        fscat = dot(hot[g][0:160], jnp.concatenate([p_high, p_low], axis=0).astype(BF16), NT)
        fscat = fscat[:, 0:128] + fscat[:, 128:256]
        for i in range(5):
            if g:
                acc[i, 0:32, :] += fscat[32 * i : 32 * i + 32]
                acc[i, 32:40, 0:32] += scat[:, 32 * i : 32 * i + 32]
            else:
                acc[i, 0:32, :] = fscat[32 * i : 32 * i + 32]
                acc[i, 32:40, :] = jnp.zeros((8, 128), F32)
                acc[i, 32:40, 0:32] = scat[:, 32 * i : 32 * i + 32]

    for copy in own[8:]:
        copy.wait()
    for s in AWAY:
        of_pos_x(s).wait_recv()
    for g in range(3):
        posmat[g][...] = jnp.zeros_like(posmat[g])
        for i in range(5):
            posmat[g][0:3, 32 * i : 32 * i + 32] = posx[i, :, 0]
    geometry(0)
    pl.when(low)(cross)
    for s in AWAY:
        of_feats(s).wait_recv()
    f_high, f_low = split2(jnp.concatenate([feats[i] for i in range(5)], axis=0))
    featt[...] = jnp.concatenate([f_high, f_low], axis=1).T.astype(BF16)
    for g in range(3):
        two = dot(featt[...], hot[g][0:160], NN)
        fbuf[g][...] = two[0:128] + two[128:256]
    main(0)

    for j in slots(1):
        of_pos_y(j).wait_recv()
    geometry(1)

    for j in slots(1):
        of_cot(j).wait_recv()
    gathered_cot(1)
    main(1)
    for j in slots(1):
        of_targets(j).start()

    for j in slots(2):
        of_pos_y(j).wait_recv()
    geometry(2)

    for p, copy in ((0, straight), (1, to_way)):
        @pl.when(place == p)
        def _(p=p, copy=copy):
            for k in range(PARTS):
                copy(k).wait_recv()
                pass_on(p, k).start()
            for k in range(PARTS):
                pass_on(p, k).wait_recv()

    one, two = slots(2)

    @pl.when(place != 0)
    def _():
        of_cot(one).wait_recv()

    @pl.when(place > 1)
    def _():
        of_cot(two).wait_recv()

    gathered_cot(2)
    main(2)
    for j in slots(2):
        of_targets(j).start()

    for s in AWAY:
        of_sums(s).start()
    pos_total = acc[2, 32:40, :] + tgt_send[2]
    feat_total = acc[2, 0:32, :]
    for s in AWAY:
        of_sums(s).wait_recv()
        feat_total = feat_total + ret[s + 2, 0:32, :]
        pos_total = pos_total + ret[s + 2, 32:40, :]
    feat_out[0, 0] = feat_total
    for s in AWAY:
        of_targets(s + 2).wait_recv()
        pos_total = pos_total + tgt_ret[s + 2]
    pos_out[:, 0] = pos_total[0:3, 0:32]

    for s in AWAY:
        of_pos_x(s).wait_send()
        of_feats(s).wait_send()
        of_sums(s).wait_send()
        of_targets(s + 2).wait_send()
    for slot in (0, 4, 1, 3):
        @pl.when(place + 2 - slot >= 0)
        def _(slot=slot):
            of_pos_y(slot).wait_send()

        @pl.when(whole(slot))
        def _(slot=slot):
            of_cot(slot).wait_send()
    for p, copy in ((run - 1, straight), (run - 2, to_way)):
        @pl.when(place == p)
        def _(copy=copy):
            for k in range(PARTS):
                copy(k).wait_send()
    for p in (0, 1):
        @pl.when(place == p)
        def _(p=p):
            for k in range(PARTS):
                pass_on(p, k).wait_send()

    for p, receivers in forwards.items():
        @pl.when(place == p)
        def _(receivers=receivers):
            for k in range(2):
                stage(k).wait_send()
                for n, (slot, shift) in enumerate(receivers):
                    forward(k, slot, n, shift).wait_send()


def local(positions, features, cotangent, nbr_src, nbr_tgt, pair_mask, pair_species, w_in, species_emb, w_out):
    hbm = pl.BlockSpec(memory_space=pltpu.HBM)
    vmem = pl.BlockSpec(memory_space=pltpu.VMEM)
    dma = pltpu.SemaphoreType.DMA

    def per_group(dtype, shape):
        return [pltpu.VMEM(shape(COUNT[g], LANES[g]), dtype) for g in range(3)]

    nbr = [x.transpose(0, 2, 3, 1, 4).reshape(25, 1, 32) for x in (nbr_src, nbr_tgt, pair_mask, pair_species)]
    xyz = positions.transpose(0, 2, 1, 3).reshape(3, 1, 32)
    pos_grad, feat_grad = pl.pallas_call(
        kernel,
        out_shape=(
            jax.ShapeDtypeStruct(xyz.shape, F32),
            jax.ShapeDtypeStruct(features.shape, F32),
        ),
        in_specs=[hbm] * 10,
        out_specs=(vmem, vmem),
        scratch_shapes=[
            pltpu.VMEM((8, 32), F32),
            pltpu.VMEM((10, 32), F32),
            pltpu.VMEM((32, 384), F32),
            pltpu.VMEM((5, 3, 1, 32), F32),
            pltpu.VMEM((5, 3, 1, 32), F32),
            pltpu.VMEM((5, 32, 128), F32),
            pltpu.VMEM((5, 32, 1152), F32),
            pltpu.VMEM((4, 25, 1, 32), jnp.int32),
            pltpu.VMEM((384, 96), BF16),
            pltpu.VMEM((32, 64), BF16),
            pltpu.VMEM((256, 160), BF16),
            pltpu.VMEM((5, 40, 128), F32),
            pltpu.VMEM((5, 8, 128), F32),
            pltpu.VMEM((5, 40, 128), F32),
            pltpu.VMEM((5, 8, 128), F32),
            pltpu.VMEM((32, 1152), F32),
            *per_group(jnp.int32, lambda n, w: (4, w)),
            *per_group(BF16, lambda n, w: (160 + 32 * n, w)),
            *per_group(F32, lambda n, w: (8, 160 + 32 * n)),
            *per_group(F32, lambda n, w: (1152, w)),
            *per_group(F32, lambda n, w: (128, w)),
            *per_group(F32, lambda n, w: (384, 2 * w)),
            *per_group(F32, lambda n, w: (8, w)),
            *per_group(F32, lambda n, w: (8, w)),
            *per_group(F32, lambda n, w: (128, w)),
            dma((11,)),
            *[dma((5,))] * 12,
            *[dma((PARTS,))] * 4,
            pltpu.SemaphoreType.REGULAR,
            dma((2,)),
            dma((2,)),
            dma((4,)),
            pltpu.VMEM((3, 1, 32), F32),
            dma((PARTS,)),
            dma((PARTS,)),
            pltpu.VMEM((32, 1152), F32),
        ],
        compiler_params=pltpu.CompilerParams(collective_id=0, has_side_effects=True, vmem_limit_bytes=56 * 2**20),
    )(xyz, features, cotangent, *nbr, w_in, species_emb, w_out)
    return pos_grad.reshape(1, 3, 1, 32).transpose(0, 2, 1, 3), feat_grad


def solution(mesh):
    grid = P("gx", "gy", None, None)
    lists = P("gx", "gy", None, None, None)
    return jax.shard_map(
        local,
        mesh=mesh,
        in_specs=(grid, grid, grid, lists, lists, lists, lists, P(), P(), P()),
        out_specs=(grid, grid),
        check_vma=False,
    )
```

```python
import math

import jax
import jax.numpy as jnp
from jax import lax
from jax.experimental import pallas as pl
from jax.experimental.pallas import tpu as pltpu
from jax.sharding import PartitionSpec as P

MESH = pl.DeviceIdType.MESH
SIDE = 5.0
CUTOFF = 12.0
SOFTEN = 0.25
F32 = jnp.float32
BF16 = jnp.bfloat16
NN = (((1,), (0,)), ((), ()))
NT = (((1,), (1,)), ((), ()))
AWAY = (-1, 1, -2, 2)
PARTS = 3
UNROLL = 16
COUNT = (1, 2, 2)
LANES = (256, 384, 384)
R3, R5, R15 = math.sqrt(3.0), math.sqrt(5.0), math.sqrt(15.0)


def dot(lhs, rhs, dims):
    return lax.dot_general(lhs, rhs, dims, preferred_element_type=F32)


def split2(value):
    high = value.astype(BF16).astype(F32)
    return high, value - high


def split3(value):
    high, rest = split2(value)
    middle, low = split2(rest)
    return high, middle, low


def sin_cos_pi(x):
    turns = jnp.floor(x + 0.5)
    y = (x - turns) * math.pi
    half = turns * 0.5
    sign = 1.0 - 4.0 * (half - jnp.floor(half))
    y2 = y * y
    s = -1.0 / 39916800.0 + y2 * (1.0 / 6227020800.0)
    for c in (1.0 / 362880.0, -1.0 / 5040.0, 1.0 / 120.0, -1.0 / 6.0, 1.0):
        s = s * y2 + c
    c_ = 1.0 / 479001600.0 - y2 * (1.0 / 87178291200.0)
    for c in (-1.0 / 3628800.0, 1.0 / 40320.0, -1.0 / 720.0, 1.0 / 24.0, -0.5, 1.0):
        c_ = c_ * y2 + c
    return s * y * sign, c_ * sign


def run_length(peers):
    return 12 if peers % 12 == 0 else 4


def remote(src, dst, send_sem, recv_sem, device):
    return pltpu.make_async_remote_copy(
        src_ref=src, dst_ref=dst, send_sem=send_sem, recv_sem=recv_sem, device_id=device, device_id_type=MESH
    )


def piece(ref, k):
    width = ref.shape[-1] // PARTS
    return ref.at[:, pl.ds(k * width, width)]


def kernel(
    pos_in, feat_in, cot_in, src_in, tgt_in, mask_in, spec_in, w_in_hbm, emb_hbm, w_out_hbm,
    sums_out,
    w_in, emb, w_out, posx, posy, feats, cots, lists, wt, w_first, featt, acc, tgt_send, ret, tgt_ret, way,
    index0, index1, index2, hot0, hot1, hot2, posmat0, posmat1, posmat2, gath0, gath1, gath2,
    fbuf0, fbuf1, fbuf2, radial0, radial1, radial2, sph0, sph1, sph2, geo0, geo1, geo2, pp0, pp1, pp2,
    local_sem, fx_send, fx_recv, py_send, py_recv, px_send, px_recv, ct_send, ct_recv,
    rs_send, rs_recv, rt_send, rt_recv, w_send, w_recv, r_send, r_recv, crossed,
    st_send, st_recv, fw_send, stage_pos, m_send, m_recv, passed,
):
    index, hot, posmat = (index0, index1, index2), (hot0, hot1, hot2), (posmat0, posmat1, posmat2)
    gath, fbuf, radial = (gath0, gath1, gath2), (fbuf0, fbuf1, fbuf2), (radial0, radial1, radial2)
    sph, geo, pp = (sph0, sph1, sph2), (geo0, geo1, geo2), (pp0, pp1, pp2)
    a, b = lax.axis_index("gx"), lax.axis_index("gy")
    na, nb = lax.axis_size("gx"), lax.axis_size("gy")
    run = run_length(nb)
    place = lax.rem(b, run)
    low = place < run // 2
    far = jnp.where(low, -1, 1)

    def x_at(shift):
        return (lax.rem(a + shift + na, na), b)

    def y_at(shift):
        return (a, lax.rem(b + shift + nb, nb))

    def slots(g):
        return [2] if g == 0 else [2 - far, 2 - 2 * far] if g == 1 else [2 + far, 2 + 2 * far]

    barrier = pltpu.get_barrier_semaphore()

    def signal(semaphore, device):
        pl.semaphore_signal(semaphore, inc=1, device_id=device, device_id_type=MESH)

    for s in AWAY:
        signal(barrier, x_at(s))
    for s in (-2, -1):
        signal(barrier, y_at(s))
    for s in (1, 2):
        @pl.when(place + s < run)
        def _(s=s):
            signal(barrier, y_at(s))

    for p, shifts in ((0, (run, run - 1, run - 2)), (1, (run, run - 2, -3))):
        @pl.when(place == p)
        def _(shifts=shifts):
            for shift in shifts:
                signal(barrier, y_at(shift))

    entered = jnp.where(place == 0, 7, jnp.where(place >= run - 2, 10, 8))

    own = [
        pltpu.make_async_copy(src, dst, local_sem.at[k])
        for k, (src, dst) in enumerate(
            (
                (src_in, lists.at[0]), (tgt_in, lists.at[1]), (mask_in, lists.at[2]), (spec_in, lists.at[3]),
                (w_out_hbm, w_out), (w_in_hbm, w_in), (emb_hbm, emb), (cot_in.at[0, 0], cots.at[2]),
                (pos_in, posx.at[2]), (pos_in, posy.at[2]), (feat_in.at[0, 0], feats.at[2]),
            )
        )
    ]
    for copy in own:
        copy.start()

    def straight(k):
        return remote(piece(cot_in.at[0, 0], k), piece(cots.at[1], k), m_send.at[k], m_recv.at[k], y_at(1))

    def to_way(k):
        return remote(piece(cot_in.at[0, 0], k), piece(passed, k), w_send.at[k], w_recv.at[k], y_at(3))

    def last():
        k = PARTS - 1
        return remote(piece(cot_in.at[0, 0], k), piece(cots.at[0], k), r_send.at[k], r_recv.at[k], y_at(2))

    def pass_on(p, k):
        src = cots.at[1] if p == 0 else passed
        return remote(piece(src, k), piece(cots.at[0], k), r_send.at[k], r_recv.at[k], y_at(1 - 2 * p))

    def of_pos_x(s):
        return remote(pos_in, posx.at[s + 2], px_send.at[s + 2], px_recv.at[s + 2], x_at(-s))

    def of_feats(s):
        return remote(feat_in.at[0, 0], feats.at[s + 2], fx_send.at[s + 2], fx_recv.at[s + 2], x_at(-s))

    def of_pos_y(slot):
        return remote(pos_in, posy.at[slot], py_send.at[slot], py_recv.at[slot], y_at(2 - slot))

    def of_cot(slot):
        return remote(cot_in.at[0, 0], cots.at[slot], ct_send.at[slot], ct_recv.at[slot], y_at(2 - slot))

    def of_sums(s):
        return remote(acc.at[s + 2], ret.at[s + 2], rs_send.at[s + 2], rs_recv.at[s + 2], x_at(s))

    def of_targets(slot):
        return remote(tgt_send.at[slot], tgt_ret.at[slot], rt_send.at[slot], rt_recv.at[slot], y_at(slot - 2))

    def gathered_cot(g):
        pieces = [split2(cots[j]) for j in slots(g)]
        stacked = jnp.concatenate([p[0] for p in pieces] + [p[1] for p in pieces], axis=0).astype(BF16)
        target_hot = hot[g][160 : 160 + 32 * COUNT[g]]
        gath[g][...] = dot(stacked.T, jnp.concatenate([target_hot, target_hot], axis=0), NN)

    def lane_maps(g):
        lane = lax.broadcasted_iota(jnp.int32, (1, LANES[g]), 1)
        second = jnp.where(lane >= 160, 1, 0)
        return lane < 160 * COUNT[g], second, (lane - 160 * second) // 32

    def setup():
        for copy in own[:8]:
            copy.wait()
        for g in range(3):
            index[g][...] = jnp.zeros_like(index[g])
            for t, j in enumerate(slots(g)):
                for i in range(5):
                    at = 160 * t + 32 * i
                    for field in range(4):
                        index[g][field : field + 1, at : at + 32] = lists[field, 5 * i + j]
            used, second, step = lane_maps(g)
            src_row = jnp.where(used, index[g][0:1] + 32 * step, -1)
            tgt_row = jnp.where(used, index[g][1:2] + 32 * second + 160, -1)
            src_ids = lax.broadcasted_iota(jnp.int32, (160, LANES[g]), 0)
            tgt_ids = lax.broadcasted_iota(jnp.int32, (32 * COUNT[g], LANES[g]), 0) + 160
            hot[g][0:160] = (src_ids == src_row).astype(F32).astype(BF16)
            hot[g][160:] = (tgt_ids == tgt_row).astype(F32).astype(BF16)
        w_high, w_low = split2(w_out[...])
        wt[...] = jnp.concatenate([w_high, w_high, w_low], axis=0).T.astype(BF16)
        i_high, i_low = split2(w_in[...])
        e_high, e_low = split2(emb[...])
        gap = jnp.zeros((6, 32), F32)
        first = [i_high, i_high, i_low, e_high, gap, e_low, gap, jnp.zeros((8, 32), F32)]
        w_first[...] = jnp.concatenate(first, axis=0).T.astype(BF16)
        gathered_cot(0)

    pl.when(low)(setup)
    pl.semaphore_wait(barrier, entered)

    @pl.when(place == run - 1)
    def _():
        signal(crossed, y_at(1 - run))
        signal(crossed, y_at(2 - run))

    @pl.when(place == run - 2)
    def _():
        signal(crossed, y_at(2 - run))

    def whole(slot):
        kept = place + 2 - slot >= 0
        if slot == 0:
            return place < run - 2
        return place < run - 1 if slot == 1 else kept

    for slot in (0, 4, 1, 3):
        @pl.when(place + 2 - slot >= 0)
        def _(slot=slot):
            of_pos_y(slot).start()
    for s in AWAY:
        of_pos_x(s).start()
    for s in AWAY:
        of_feats(s).start()
    @pl.when(place == run - 1)
    def _():
        for k in range(PARTS - 1):
            straight(k).start()
        last().start()
        straight(PARTS - 1).start()

    @pl.when(place == run - 2)
    def _():
        for k in range(PARTS - 1):
            to_way(k).start()
        last().start()

    for slot in (1, 3, 0, 4):
        @pl.when(whole(slot))
        def _(slot=slot):
            of_cot(slot).start()

    def stage(k):
        src, dst = ((pos_in, stage_pos), (cot_in.at[0, 0], way))[k]
        return remote(src, dst, st_send.at[k], st_recv.at[k], y_at(-run))

    def forward(k, slot, n, shift):
        src, dst = ((stage_pos, posy.at[slot]), (way, cots.at[slot]))[k]
        return remote(src, dst, fw_send.at[2 * n + k], (py_recv, ct_recv)[k].at[slot], y_at(shift))

    forwards = {0: ((3, run - 1), (4, run - 2)), 1: ((4, run - 2),)}

    @pl.when(place <= 1)
    def _():
        stage(0).start()
        stage(1).start()

    def cross():
        for p, receivers in forwards.items():
            @pl.when(place == p)
            def _(receivers=receivers):
                pl.semaphore_wait(crossed, len(receivers))
                for k in range(2):
                    stage(k).wait_recv()
                    for n, (slot, shift) in enumerate(receivers):
                        forward(k, slot, n, shift).start()

    pl.when(jnp.logical_not(low))(setup)

    def geometry(g):
        width = LANES[g]
        for t, j in enumerate(slots(g)):
            posmat[g][0:3, 160 + 32 * t : 192 + 32 * t] = -posy[j, :, 0]
        picked = dot(jnp.concatenate(split3(posmat[g][...]), axis=0).astype(BF16), hot[g][...], NN)
        picked = picked[0:8] + picked[8:16] + picked[16:24]
        used, second, step = lane_maps(g)
        rx = picked[0:1] + (step - 2).astype(F32) * SIDE
        ry, rz = picked[1:2], picked[2:3]
        if g:
            ry = ry - ((far if g == 2 else -far) * (1 + second)).astype(F32) * SIDE
        dist = jnp.sqrt(rx * rx + ry * ry + rz * rz + SOFTEN)
        inv = 1.0 / dist
        ux, uy, uz = rx * inv, ry * inv, rz * inv
        q = dist * (1.0 / CUTOFF)
        left = jnp.maximum(1.0 - q * q, 0.0)
        alive = index[g][2:3].astype(F32)
        env = left * left * alive
        denv = q * left * alive * (-4.0 / CUTOFF)
        sph[g][...] = jnp.concatenate(
            [
                R3 * ux, R3 * uy, R3 * uz,
                R15 * ux * uy, R15 * uy * uz, 0.5 * R5 * (2.0 * uz * uz - ux * ux - uy * uy),
                R15 * ux * uz, 0.5 * R15 * (ux * ux - uy * uy),
            ],
            axis=0,
        )
        geo[g][0:4] = jnp.concatenate([ux, uy, uz, inv], axis=0)
        order = (lax.broadcasted_iota(jnp.int32, (8, width), 0) + 1).astype(F32)
        root = math.sqrt(2.0 / CUTOFF)
        sine, cosine = sin_cos_pi(order * q)
        basis = root * sine * inv
        dbasis = (order * (root * math.pi / CUTOFF) * cosine - basis) * inv
        chosen = (lax.broadcasted_iota(jnp.int32, (16, width), 0) == index[g][3:4]).astype(F32)
        chosen = jnp.concatenate([chosen, jnp.zeros_like(chosen)], axis=1)
        high, rest = split2(jnp.concatenate([basis, dbasis], axis=1))
        first = jnp.concatenate([high, rest, high, chosen, chosen, jnp.zeros_like(high)], axis=0)
        both = dot(w_first[...], first.astype(BF16), NN)
        z, dz = both[:, :width], both[:, width:]
        sig = 1.0 / (1.0 + jnp.exp(-z))
        hidden = z * sig
        dhidden = sig * (1.0 + z * (1.0 - sig)) * dz
        high, rest = split2(jnp.concatenate([hidden * env, dhidden * env + hidden * denv], axis=1))
        radial[g][...] = dot(wt[...], jnp.concatenate([high, rest, high], axis=0).astype(BF16), NN)

    def main(g):
        width = LANES[g]
        columns = []
        for block in range(width // 128):
            at = 128 * block
            lanes = pl.ds(at, 128)

            def channels(c, carry, at=at, lanes=lanes):
                carry = list(carry)
                products = []
                for u in range(UNROLL):
                    r0 = pl.multiple_of(c * (8 * UNROLL) + u * 8, 8)
                    f = fbuf[g][pl.ds(r0, 8), lanes]
                    w = [gath[g][pl.ds(m * 128 + r0, 8), lanes] for m in range(9)]
                    y = [None] + [sph[g][m : m + 1, lanes] for m in range(8)]
                    rad = [radial[g][pl.ds(l * 128 + r0, 8), lanes] for l in range(3)]
                    drad = [radial[g][pl.ds(l * 128 + r0, 8), pl.ds(width + at, 128)] for l in range(3)]
                    c1 = y[1] * w[1] + y[2] * w[2] + y[3] * w[3]
                    c2 = (y[4] * w[4] + y[5] * w[5]) + (y[6] * w[6] + y[7] * w[7]) + y[8] * w[8]
                    products.append(rad[0] * w[0] + rad[1] * c1 + rad[2] * c2)
                    p1, p2 = rad[1] * f, rad[2] * f
                    carry[0] = carry[0] + f * (drad[0] * w[0] + drad[1] * c1 + drad[2] * c2)
                    for m in range(1, 9):
                        carry[m] = carry[m] + (p1 if m < 4 else p2) * w[m]
                for u in range(UNROLL):
                    pp[g][pl.ds(pl.multiple_of(c * (8 * UNROLL) + u * 8, 8), 8), lanes] = products[u]
                return tuple(carry)

            sums = lax.fori_loop(0, 16 // UNROLL, channels, tuple(jnp.zeros((8, 128), F32) for _ in range(9)))
            columns.append([jnp.sum(v, axis=0, keepdims=True) for v in sums])
        gd, *gy = [jnp.concatenate([column[m] for column in columns], axis=1) for m in range(9)]
        ux, uy, uz, inv = (geo[g][k : k + 1] for k in range(4))
        gux = R3 * gy[0] + R15 * (uy * gy[3] + uz * gy[6] + ux * gy[7]) - R5 * ux * gy[5]
        guy = R3 * gy[1] + R15 * (ux * gy[3] + uz * gy[4] - uy * gy[7]) - R5 * uy * gy[5]
        guz = R3 * gy[2] + R15 * (uy * gy[4] + ux * gy[6]) + 2.0 * R5 * uz * gy[5]
        along = gd - (gux * ux + guy * uy + guz * uz) * inv
        grad = jnp.concatenate(
            [gux * inv + along * ux, guy * inv + along * uy, guz * inv + along * uz, jnp.zeros((5, width), F32)], axis=0
        )
        scat = dot(jnp.concatenate(split2(grad), axis=0).astype(BF16), hot[g][...], NT)
        scat = scat[0:8] + scat[8:16]
        for t, j in enumerate(slots(g)):
            tgt_send[j, :, 0:32] = -scat[:, 160 + 32 * t : 192 + 32 * t]
        p_high, p_low = split2(pp[g][...])
        fscat = dot(hot[g][0:160], jnp.concatenate([p_high, p_low], axis=0).astype(BF16), NT)
        fscat = fscat[:, 0:128] + fscat[:, 128:256]
        for i in range(5):
            if g:
                acc[i, 0:32, :] += fscat[32 * i : 32 * i + 32]
                acc[i, 32:40, 0:32] += scat[:, 32 * i : 32 * i + 32]
            else:
                acc[i, 0:32, :] = fscat[32 * i : 32 * i + 32]
                acc[i, 32:40, :] = jnp.zeros((8, 128), F32)
                acc[i, 32:40, 0:32] = scat[:, 32 * i : 32 * i + 32]

    for copy in own[8:]:
        copy.wait()
    for s in AWAY:
        of_pos_x(s).wait_recv()
    for g in range(3):
        posmat[g][...] = jnp.zeros_like(posmat[g])
        for i in range(5):
            posmat[g][0:3, 32 * i : 32 * i + 32] = posx[i, :, 0]
    geometry(0)
    pl.when(low)(cross)
    for s in AWAY:
        of_feats(s).wait_recv()
    f_high, f_low = split2(jnp.concatenate([feats[i] for i in range(5)], axis=0))
    featt[...] = jnp.concatenate([f_high, f_low], axis=1).T.astype(BF16)
    for g in range(3):
        two = dot(featt[...], hot[g][0:160], NN)
        fbuf[g][...] = two[0:128] + two[128:256]
    main(0)

    for j in slots(1):
        of_pos_y(j).wait_recv()
    geometry(1)

    for j in slots(1):
        of_cot(j).wait_recv()
    gathered_cot(1)
    main(1)
    for j in slots(1):
        of_targets(j).start()

    for j in slots(2):
        of_pos_y(j).wait_recv()
    geometry(2)

    for p, copy in ((0, straight), (1, to_way)):
        @pl.when(place == p)
        def _(p=p, copy=copy):
            for k in range(PARTS - 1):
                copy(k).wait_recv()
                pass_on(p, k).start()
            if p == 0:
                straight(PARTS - 1).wait_recv()
            for k in range(PARTS - 1):
                pass_on(p, k).wait_recv()
            last().wait_recv()

    one, two = slots(2)

    @pl.when(place != 0)
    def _():
        of_cot(one).wait_recv()

    @pl.when(place > 1)
    def _():
        of_cot(two).wait_recv()

    gathered_cot(2)
    main(2)
    for j in slots(2):
        of_targets(j).start()

    for s in AWAY:
        of_sums(s).start()
    pos_total = acc[2, 32:40, :] + tgt_send[2]
    feat_total = acc[2, 0:32, :]
    for s in AWAY:
        of_sums(s).wait_recv()
        feat_total = feat_total + ret[s + 2, 0:32, :]
        pos_total = pos_total + ret[s + 2, 32:40, :]
    sums_out[0:32] = feat_total
    for s in AWAY:
        of_targets(s + 2).wait_recv()
        pos_total = pos_total + tgt_ret[s + 2]
    sums_out[32:40] = pos_total

    for s in AWAY:
        of_pos_x(s).wait_send()
        of_feats(s).wait_send()
        of_sums(s).wait_send()
        of_targets(s + 2).wait_send()
    for slot in (0, 4, 1, 3):
        @pl.when(place + 2 - slot >= 0)
        def _(slot=slot):
            of_pos_y(slot).wait_send()

        @pl.when(whole(slot))
        def _(slot=slot):
            of_cot(slot).wait_send()
    for p, copy, count in ((run - 1, straight, PARTS), (run - 2, to_way, PARTS - 1)):
        @pl.when(place == p)
        def _(copy=copy, count=count):
            for k in range(count):
                copy(k).wait_send()
            last().wait_send()
    for p in (0, 1):
        @pl.when(place == p)
        def _(p=p):
            for k in range(PARTS - 1):
                pass_on(p, k).wait_send()

    for p, receivers in forwards.items():
        @pl.when(place == p)
        def _(receivers=receivers):
            for k in range(2):
                stage(k).wait_send()
                for n, (slot, shift) in enumerate(receivers):
                    forward(k, slot, n, shift).wait_send()


def split(sums, pos_out, feat_out):
    feat_out[0, 0] = sums[0:32]
    pos_out[:, 0] = sums[32:35, 0:32]


def local(positions, features, cotangent, nbr_src, nbr_tgt, pair_mask, pair_species, w_in, species_emb, w_out):
    hbm = pl.BlockSpec(memory_space=pltpu.HBM)
    vmem = pl.BlockSpec(memory_space=pltpu.VMEM)
    dma = pltpu.SemaphoreType.DMA

    def per_group(dtype, shape):
        return [pltpu.VMEM(shape(COUNT[g], LANES[g]), dtype) for g in range(3)]

    nbr = [x.transpose(0, 2, 3, 1, 4).reshape(25, 1, 32) for x in (nbr_src, nbr_tgt, pair_mask, pair_species)]
    xyz = positions.transpose(0, 2, 1, 3).reshape(3, 1, 32)
    sums = pl.pallas_call(
        kernel,
        out_shape=jax.ShapeDtypeStruct((40, 128), F32),
        in_specs=[hbm] * 10,
        out_specs=vmem,
        scratch_shapes=[
            pltpu.VMEM((8, 32), F32),
            pltpu.VMEM((10, 32), F32),
            pltpu.VMEM((32, 384), F32),
            pltpu.VMEM((5, 3, 1, 32), F32),
            pltpu.VMEM((5, 3, 1, 32), F32),
            pltpu.VMEM((5, 32, 128), F32),
            pltpu.VMEM((5, 32, 1152), F32),
            pltpu.VMEM((4, 25, 1, 32), jnp.int32),
            pltpu.VMEM((384, 96), BF16),
            pltpu.VMEM((32, 64), BF16),
            pltpu.VMEM((256, 160), BF16),
            pltpu.VMEM((5, 40, 128), F32),
            pltpu.VMEM((5, 8, 128), F32),
            pltpu.VMEM((5, 40, 128), F32),
            pltpu.VMEM((5, 8, 128), F32),
            pltpu.VMEM((32, 1152), F32),
            *per_group(jnp.int32, lambda n, w: (4, w)),
            *per_group(BF16, lambda n, w: (160 + 32 * n, w)),
            *per_group(F32, lambda n, w: (8, 160 + 32 * n)),
            *per_group(F32, lambda n, w: (1152, w)),
            *per_group(F32, lambda n, w: (128, w)),
            *per_group(F32, lambda n, w: (384, 2 * w)),
            *per_group(F32, lambda n, w: (8, w)),
            *per_group(F32, lambda n, w: (8, w)),
            *per_group(F32, lambda n, w: (128, w)),
            dma((11,)),
            *[dma((5,))] * 12,
            *[dma((PARTS,))] * 4,
            pltpu.SemaphoreType.REGULAR,
            dma((2,)),
            dma((2,)),
            dma((4,)),
            pltpu.VMEM((3, 1, 32), F32),
            dma((PARTS,)),
            dma((PARTS,)),
            pltpu.VMEM((32, 1152), F32),
        ],
        compiler_params=pltpu.CompilerParams(collective_id=0, has_side_effects=True, vmem_limit_bytes=56 * 2**20),
    )(xyz, features, cotangent, *nbr, w_in, species_emb, w_out)
    pos_grad, feat_grad = pl.pallas_call(
        split,
        out_shape=(jax.ShapeDtypeStruct(xyz.shape, F32), jax.ShapeDtypeStruct(features.shape, F32)),
        in_specs=[vmem],
        out_specs=(vmem, vmem),
    )(sums)
    return pos_grad.reshape(1, 3, 1, 32).transpose(0, 2, 1, 3), feat_grad


def solution(mesh):
    grid = P("gx", "gy", None, None)
    lists = P("gx", "gy", None, None, None)
    return jax.shard_map(
        local,
        mesh=mesh,
        in_specs=(grid, grid, grid, lists, lists, lists, lists, P(), P(), P()),
        out_specs=(grid, grid),
        check_vma=False,
    )
```
